256 devices in a mesh: pair: 64 (over y, z, core), virt: 4 (over x).
Axes of the slice: x: 4, y: 4, z: 8, core: 2. Of those that a mesh axis runs over, the one named last changes fastest.
Arguments:
- amplitudes: bfloat16 [2048, 128, 1024], P('pair', 'virt'), may hold values from -6 to 6
- amp_pairs: int32 [2048], P('pair'), may hold values from 0 to 16383, as said below
- pair_map: int32 [16384], replicated, may hold values from -1 to 511, as said below
- integrals: bfloat16 [512, 2, 1024, 1024], P('pair', None, None, 'virt'), may hold values from -0.1875 to 0.1875
- block_cols: int32 [512, 2], P('pair'), may hold values from 0 to 16383, as said below
- occ_energy: float32 [8192], P('pair'), may hold values from -3 to -0.7
- virt_energy: float32 [4096], replicated, may hold values from 0.3 to 2
Outputs:
- update: bfloat16 [2048, 128, 1024], P('pair', None, 'virt')
The draws below stay inside these ranges and needn't reach their ends.
Inputs may be any that keep to these rules, and one draw needn't show every extreme that they name: `amp_pairs`: within one occupied tile (tiles k * 32 to k * 32 + 31) the pairs differ and each has a row in pair_map. Consecutive occupied tiles form groups that hold the same set of pairs, and a pair belongs to one group only. `pair_map`: exactly 512 entries are not -1: the rows 0 to 511, once each, at the pairs that occur in amp_pairs. Row u lies on pair index u // 8. The pairs of one occupied tile have at most 1 row on any one pair index, and some reach 1. At most 8 occupied tiles hold the pair of any one row, and some row is held by exactly 8. `block_cols`: the 2 entries of a row differ, and each is a pair of the group of occupied tiles that holds the row's own pair.
All inputs are finite; a program needn't handle non-finite values.
Results may differ from the reference program's by a relative error of at most 0.0049.
Values may be sent and summed in bfloat16 or wider, within the bound.
A program may use at most 128 MiB of HBM per device.

```python
import jax
import jax.numpy as jnp
from jax import lax

VIRT = 4096
VTILE = 32
TILE_O = 128
MQ = 2
AT_DEV = 32
VT = 128
NVP = 16384
VPAIR = 1024
RB_DEV = 8
NROW = 512
NAMP = 2048
NOCC = 8192
NCL = 16
KMAX = 8
N_PAIR = 64


def layout(key):
    subkeys = [jax.random.fold_in(key, 9100 + offset) for offset in range(6)]
    spare_slots = (NCL - 1) * (KMAX - 1)
    leftover = N_PAIR - NCL - (KMAX - 1)
    slot_order = jax.random.permutation(subkeys[0], spare_slots)
    extras = jnp.sum((slot_order < leftover).astype(jnp.int32).reshape(NCL - 1, KMAX - 1), axis=1)
    full_group = jax.random.randint(subkeys[1], (), 0, NCL)
    group_index = jnp.arange(NCL, dtype=jnp.int32)
    other_index = jnp.clip(group_index - (group_index > full_group).astype(jnp.int32), 0, NCL - 2)
    group_sizes = jnp.where(group_index == full_group, KMAX, 1 + extras[other_index]).astype(jnp.int32)
    group_starts = jnp.cumsum(group_sizes) - group_sizes
    otile_index = jnp.arange(N_PAIR, dtype=jnp.int32)
    group_of_otile = jnp.sum((otile_index[:, None] >= group_starts[None, 1:]).astype(jnp.int32), axis=1)
    owner_order = jax.random.permutation(subkeys[2], N_PAIR).astype(jnp.int32)
    owner_inverse = jnp.argsort(owner_order).astype(jnp.int32)

    def row_of_position(position):
        return owner_order[position % N_PAIR] * RB_DEV + position // N_PAIR
    tile_scores = jax.random.randint(subkeys[3], (N_PAIR, AT_DEV), 0, 1 << 20) * AT_DEV + jnp.arange(AT_DEV, dtype=jnp.int32)[None, :]
    tile_perm = jnp.argsort(tile_scores, axis=1).astype(jnp.int32)
    positions = group_of_otile[:, None] * AT_DEV + tile_perm
    pair_of_row = jax.random.permutation(subkeys[4], NVP)[:NROW].astype(jnp.int32)
    amp_pairs = pair_of_row[row_of_position(positions)].reshape(NAMP)
    pair_map = jnp.full((NVP,), -1, jnp.int32).at[pair_of_row].set(jnp.arange(NROW, dtype=jnp.int32))
    row_ids = jnp.arange(NROW, dtype=jnp.int32)
    row_position = row_ids % RB_DEV * N_PAIR + owner_inverse[row_ids // RB_DEV]
    row_group = row_position // AT_DEV
    col_scores = jax.random.randint(subkeys[5], (NROW, AT_DEV), 0, 1 << 20) * AT_DEV + jnp.arange(AT_DEV, dtype=jnp.int32)[None, :]
    col_values, col_choice = lax.top_k(col_scores, MQ)
    block_cols = pair_of_row[row_of_position(row_group[:, None] * AT_DEV + col_choice.astype(jnp.int32))]
    return (amp_pairs.astype(jnp.int32), pair_map, block_cols.astype(jnp.int32))


def draw_amp_pairs(key, part):
    return layout(key)[0]


def draw_pair_map(key, part):
    return layout(key)[1]


def draw_block_cols(key, part):
    return layout(key)[2]


def shard_levels(rng, extent, split, low, high):
    gain, own = 1.0, jax.random.fold_in(rng, 6)
    for dim, blocks in split:
        steps = jnp.exp(jax.random.uniform(jax.random.fold_in(own, dim), (blocks,), jnp.float32, low / len(split), high / len(split)))
        gain = gain * jnp.repeat(steps, extent[dim] // blocks).reshape([-1 if axis == dim else 1 for axis in range(len(extent))])
    return gain


def gaussian(own_key, extent, width, limit, pieces=(), kind=jnp.bfloat16):
    result = width * jax.random.normal(own_key, extent, jnp.float32)
    if pieces:
        result = result * shard_levels(own_key, extent, pieces, -0.22, 0.18)
    return jnp.clip(result, -limit, limit).astype(kind)


def setup_inputs(seed: int = 0) -> dict:
    key_of = jax.random.split(jax.random.key(seed), 8)
    return {
        "amplitudes": gaussian(key_of[0], (NAMP, TILE_O, VPAIR), 1.0, 6.0, ((0, 64), (1, 4))),
        "amp_pairs": draw_amp_pairs(jax.random.fold_in(key_of[7], 71), 0),
        "pair_map": draw_pair_map(jax.random.fold_in(key_of[7], 71), 0),
        "integrals": gaussian(key_of[3], (NROW, MQ, VPAIR, VPAIR), VPAIR ** -0.5, 0.1875, ((0, 64), (3, 4))),
        "block_cols": draw_block_cols(jax.random.fold_in(key_of[7], 71), 0),
        "occ_energy": jnp.clip(-3.0 + 2.3 * jax.random.uniform(key_of[5], (NOCC,), jnp.float32) ** shard_levels(key_of[5], (NOCC,), ((0, 64),), -0.2, 0.2), -3.0, -0.7),
        "virt_energy": jnp.clip(jax.random.uniform(key_of[6], (VIRT,), jnp.float32, 0.3, 2.0), 0.3, 2.0),
    }


def reference(amplitudes, amp_pairs, pair_map, integrals, block_cols, occ_energy, virt_energy):
    tile_rows = pair_map[amp_pairs]
    energy_table = virt_energy.reshape(VT, VTILE)

    def one_otile(otile_index):
        first_tile = otile_index * AT_DEV
        tile_set = lax.dynamic_slice_in_dim(amplitudes, first_tile, AT_DEV, 0)
        pair_ids = lax.dynamic_slice_in_dim(amp_pairs, first_tile, AT_DEV, 0)
        rows_here = lax.dynamic_slice_in_dim(tile_rows, first_tile, AT_DEV, 0)

        def product_step(running, tile_slot):
            row_id = rows_here[tile_slot]
            present = row_id >= 0
            safe_row = jnp.maximum(row_id, 0)
            block_set = integrals[safe_row].astype(jnp.float32)
            one_tile = tile_set[tile_slot].astype(jnp.float32)
            partial_tile = jnp.einsum("id,mdc->mic", one_tile, block_set)
            rounded = lax.optimization_barrier(partial_tile.astype(jnp.bfloat16)).astype(jnp.float32)
            columns = block_cols[safe_row]
            landing = ((pair_ids[None, :] == columns[:, None]) & present).astype(jnp.float32)
            return running + jnp.einsum("ma,mic->aic", landing, rounded), None

        start_total = jnp.zeros((AT_DEV, TILE_O, VPAIR), jnp.float32)
        ladder, _ = lax.scan(product_step, start_total, jnp.arange(AT_DEV, dtype=jnp.int32))
        occ_here = lax.dynamic_slice_in_dim(occ_energy, otile_index * TILE_O, TILE_O, 0)
        energy_first = energy_table[pair_ids // VT]
        energy_second = energy_table[pair_ids % VT]
        denominator = energy_first[:, None, :, None] + energy_second[:, None, None, :] - occ_here[None, :, None, None]
        return (ladder / denominator.reshape(AT_DEV, TILE_O, VPAIR)).astype(jnp.bfloat16)

    blocks_out = lax.map(one_otile, jnp.arange(N_PAIR, dtype=jnp.int32))
    return blocks_out.reshape(NAMP, TILE_O, VPAIR)
```

```python
import functools

import jax
import jax.numpy as jnp
from jax import lax
from jax.experimental import pallas as pl
from jax.experimental.pallas import tpu as pltpu
from jax.sharding import PartitionSpec as P

VTILE = 32
MESH = pl.DeviceIdType.MESH
LANES = 128
LAG_RELAY, LAG_DOT, LAG_SEND = 3, 6, 7


def plan_kernel(local_rows, pair_map, amp_pairs, block_cols, tile_of_slot, meta):
    slots = tile_of_slot.shape[0]

    def clear(d, carry):
        tile_of_slot[d] = 0
        meta[0, 0, d] = -1
        return carry

    lax.fori_loop(0, slots, clear, 0)

    def place(j, carry):
        row = pair_map[amp_pairs[j]]

        @pl.when(row >= 0)
        def _():
            owner = lax.div(row, local_rows)
            tile_of_slot[owner] = j
            meta[0, 0, owner] = lax.rem(row, local_rows)

        return carry

    lax.fori_loop(0, amp_pairs.shape[0], place, 0)

    def copy(i, carry):
        meta[0, 0, slots + i] = block_cols[i]
        return carry

    lax.fori_loop(0, block_cols.shape[0], copy, 0)


def exchange_kernel(
    dims,
    tile_of_slot,
    meta_in,
    amplitudes,
    integrals,
    returned,
    meta_all,
    slots,
    gathered,
    blocks,
    products,
    meta_table,
    amp_send,
    amp_recv,
    right_send,
    left_send,
    relay_right_send,
    relay_left_send,
    from_left,
    from_right,
    relay_from_left,
    relay_from_right,
    product_send,
    product_recv,
    meta_send,
    meta_recv,
    load_sem,
):
    ny, nz, nc = dims
    n = ny * nz * nc
    me = lax.axis_index("pair")
    col = lax.axis_index("virt")
    nv = gathered.shape[1]
    height = gathered.shape[2]
    half = height // 2
    right, left, across = lax.rem(col + 1, nv), lax.rem(col + nv - 1, nv), lax.rem(col + 2, nv)
    my_y, my_z, my_c = lax.div(me, nz * nc), lax.rem(lax.div(me, nc), nz), lax.rem(me, nc)

    def partner(k, sign):
        i = lax.rem(k, nz)
        t = lax.div(i + 1, 2)
        odd = lax.rem(i, 2)
        dz = odd * t + (1 - odd) * lax.rem(nz - t, nz)
        dy = lax.rem(lax.div(k, nz), ny)
        dc = lax.div(k, nz * ny)
        y = lax.rem(my_y + sign * dy + ny, ny)
        z = lax.rem(my_z + sign * dz + nz, nz)
        c = lax.rem(my_c + dc, nc)
        return (y * nz + z) * nc + c

    def wait(ref, sem):
        pltpu.make_async_copy(ref, ref, sem).wait()

    load = pltpu.make_async_copy(integrals, blocks, load_sem)
    load.start()

    def fill(d, carry):
        slots[d] = amplitudes[tile_of_slot[d]]
        return carry

    lax.fori_loop(0, n, fill, 0)

    barrier = pltpu.get_barrier_semaphore()

    def greet(k, carry):
        pl.semaphore_signal(barrier, inc=1, device_id=(partner(k, 1), col), device_id_type=MESH)
        return carry

    lax.fori_loop(1, n, greet, 0)
    pl.semaphore_signal(barrier, inc=1, device_id=(me, right), device_id_type=MESH)
    pl.semaphore_signal(barrier, inc=1, device_id=(me, left), device_id_type=MESH)
    pl.semaphore_wait(barrier, n + 1)

    def send_meta(k, carry):
        pltpu.make_async_remote_copy(
            src_ref=meta_in.at[0],
            dst_ref=meta_all.at[me],
            send_sem=meta_send,
            recv_sem=meta_recv,
            device_id=(partner(k, 1), col),
            device_id_type=MESH,
        ).start()
        return carry

    lax.fori_loop(1, n, send_meta, 0)
    pltpu.make_async_copy(meta_in.at[0], meta_all.at[me], meta_recv).start()
    pltpu.make_async_copy(slots.at[me], gathered.at[me, col], amp_recv.at[0]).start()

    def send_slot(k, carry):
        target = partner(k, 1)
        pltpu.make_async_remote_copy(
            src_ref=slots.at[target],
            dst_ref=gathered.at[me, col],
            send_sem=amp_send,
            recv_sem=amp_recv.at[k],
            device_id=(target, col),
            device_id_type=MESH,
        ).start()
        return carry

    lax.fori_loop(1, n, send_slot, 0)

    wait(meta_all, meta_recv)
    table = pltpu.make_async_copy(meta_all, meta_table, load_sem)
    load.wait()
    table.start()
    table.wait()

    def along(ref, send_sem, recv_sem, target):
        pltpu.make_async_remote_copy(
            src_ref=ref,
            dst_ref=ref,
            send_sem=send_sem,
            recv_sem=recv_sem,
            device_id=(me, target),
            device_id_type=MESH,
        ).start()

    def step(t, carry):
        @pl.when(t < n)
        def _():
            own = gathered.at[partner(t, -1), col]
            wait(own, amp_recv.at[t])
            along(own, right_send, from_left.at[t], right)
            along(own, left_send, from_right.at[t], left)

        @pl.when((t >= LAG_RELAY) & (t < n + LAG_RELAY))
        def _():
            u = t - LAG_RELAY
            source = partner(u, -1)
            wait(gathered.at[source, left], from_left.at[u])
            along(
                gathered.at[source, left, pl.ds(0, half)], relay_right_send, relay_from_left.at[u], right
            )
            wait(gathered.at[source, right], from_right.at[u])
            along(
                gathered.at[source, right, pl.ds(half, half)], relay_left_send, relay_from_right.at[u], left
            )

        @pl.when((t >= LAG_DOT) & (t < n + LAG_DOT))
        def _():
            u = t - LAG_DOT
            source = partner(u, -1)
            wait(gathered.at[source, across, pl.ds(0, half)], relay_from_left.at[u])
            wait(gathered.at[source, across, pl.ds(half, half)], relay_from_right.at[u])
            row = jnp.maximum(meta_table[source, 0, me], 0)
            tile = gathered[source].reshape(nv * height, gathered.shape[3])
            for m in range(blocks.shape[1]):
                products[u, m] = jnp.dot(
                    tile, blocks[row, m], preferred_element_type=jnp.float32
                ).astype(jnp.bfloat16)

        @pl.when(t == LAG_SEND)
        def _():
            pltpu.make_async_copy(products.at[0], returned.at[me], product_recv).start()

        @pl.when(t > LAG_SEND)
        def _():
            u = t - LAG_SEND
            pltpu.make_async_remote_copy(
                src_ref=products.at[u],
                dst_ref=returned.at[me],
                send_sem=product_send,
                recv_sem=product_recv,
                device_id=(partner(u, -1), col),
                device_id_type=MESH,
            ).start()

        return carry

    lax.fori_loop(0, n + LAG_SEND, step, 0)

    wait(meta_all.at[pl.ds(0, n - 1)], meta_send)
    wait(slots.at[pl.ds(0, n - 1)], amp_send)
    wait(slots, right_send)
    wait(slots, left_send)
    wait(slots.at[pl.ds(0, n // 2)], relay_right_send)
    wait(slots.at[pl.ds(0, n // 2)], relay_left_send)
    wait(products.at[pl.ds(0, n - 1)], product_send)
    wait(returned, product_recv)


def combine_kernel(
    virt_tiles, amp_pairs, my_meta, meta_all, returned, first_table, second_table, occ, update, position, ladder
):
    step = pl.program_id(0)
    chunk = returned.shape[0]
    slots = meta_all.shape[0]

    @pl.when(step == 0)
    def _():
        def mark(j, carry):
            position[amp_pairs[j]] = j
            return carry

        lax.fori_loop(0, amp_pairs.shape[0], mark, 0)
        ladder[...] = jnp.zeros_like(ladder)

    def add(i, carry):
        slot = step * chunk + i
        row = my_meta[0, 0, slot]

        @pl.when(row >= 0)
        def _():
            for m in range(returned.shape[1]):
                target = position[meta_all[slot, 0, slots + row * returned.shape[1] + m]]
                ladder[target] += returned[i, m].astype(jnp.float32)

        return carry

    lax.fori_loop(0, chunk, add, 0)

    @pl.when(step == pl.num_programs(0) - 1)
    def _():
        def divide(j, carry):
            pair = amp_pairs[j]
            energy = (
                first_table[pl.ds(lax.div(pair, virt_tiles), 1), :]
                + second_table[pl.ds(lax.rem(pair, virt_tiles), 1), :]
            )
            update[j] = (ladder[j] / (energy - occ[...])).astype(update.dtype)
            return carry

        lax.fori_loop(0, amp_pairs.shape[0], divide, 0)


def pair_dims(n):
    return {64: (4, 8, 2), 8: (2, 2, 2), 4: (1, 2, 2)}[n]


def local(amplitudes, amp_pairs, pair_map, integrals, block_cols, occ_energy, virt_energy):
    tile_count, height, full_width = amplitudes.shape
    n = lax.axis_size("pair")
    nv = lax.axis_size("virt")
    local_rows, block_count, _, part_width = integrals.shape
    occ_rows = occ_energy.shape[0]
    smem = pl.BlockSpec(memory_space=pltpu.SMEM)
    vmem = pl.BlockSpec(memory_space=pltpu.VMEM)
    hbm = pl.BlockSpec(memory_space=pl.ANY)

    tile_of_slot, my_meta = pl.pallas_call(
        functools.partial(plan_kernel, local_rows),
        out_shape=(
            jax.ShapeDtypeStruct((n,), jnp.int32),
            jax.ShapeDtypeStruct((1, 1, LANES), jnp.int32),
        ),
        in_specs=[smem] * 3,
        out_specs=(smem, smem),
        name="plan",
    )(pair_map, amp_pairs, block_cols.reshape(-1))

    dma = pltpu.SemaphoreType.DMA
    returned, meta_all = pl.pallas_call(
        functools.partial(exchange_kernel, pair_dims(n)),
        out_shape=(
            jax.ShapeDtypeStruct((n, block_count, occ_rows, part_width), jnp.bfloat16),
            jax.ShapeDtypeStruct((n, 1, LANES), jnp.int32),
        ),
        in_specs=[smem, vmem, vmem, hbm],
        out_specs=(hbm, hbm),
        scratch_shapes=[
            pltpu.VMEM((n, height, full_width), jnp.bfloat16),
            pltpu.VMEM((n, nv, height, full_width), jnp.bfloat16),
            pltpu.VMEM(integrals.shape, jnp.bfloat16),
            pltpu.VMEM((n, block_count, occ_rows, part_width), jnp.bfloat16),
            pltpu.SMEM((n, 1, LANES), jnp.int32),
            dma,
            dma((n,)),
            dma,
            dma,
            dma,
            dma,
            dma((n,)),
            dma((n,)),
            dma((n,)),
            dma((n,)),
            dma,
            dma,
            dma,
            dma,
            dma,
        ],
        compiler_params=pltpu.CompilerParams(
            collective_id=0, has_side_effects=True, vmem_limit_bytes=60 * 2**20
        ),
        name="exchange",
    )(tile_of_slot, my_meta, amplitudes, integrals)

    virt_tiles = virt_energy.shape[0] // VTILE
    energy_table = virt_energy.reshape(virt_tiles, VTILE)
    per_device = VTILE // nv
    first = lax.dynamic_slice_in_dim(
        energy_table, lax.axis_index("virt") * per_device, per_device, 1
    )
    first_table = jnp.repeat(first, VTILE, axis=1)
    second_table = jnp.tile(energy_table, (1, per_device))
    chunk = min(8, n)
    whole = lambda *shape: pl.BlockSpec(shape, lambda i: (0,) * len(shape))
    return pl.pallas_call(
        functools.partial(combine_kernel, virt_tiles),
        out_shape=jax.ShapeDtypeStruct((tile_count, occ_rows, part_width), jnp.bfloat16),
        grid=(n // chunk,),
        in_specs=[
            smem,
            smem,
            smem,
            pl.BlockSpec((chunk, block_count, occ_rows, part_width), lambda i: (i, 0, 0, 0)),
            whole(virt_tiles, part_width),
            whole(virt_tiles, part_width),
            whole(occ_rows, 1),
        ],
        out_specs=whole(tile_count, occ_rows, part_width),
        scratch_shapes=[
            pltpu.SMEM((pair_map.shape[0],), jnp.int32),
            pltpu.VMEM((tile_count, occ_rows, part_width), jnp.float32),
        ],
        compiler_params=pltpu.CompilerParams(vmem_limit_bytes=32 * 2**20),
        name="combine",
    )(amp_pairs, my_meta, meta_all, returned, first_table, second_table, occ_energy[:, None])


def solution(mesh):
    in_specs = (
        P("pair", "virt", None),
        P("pair"),
        P(),
        P("pair", None, None, "virt"),
        P("pair", None),
        P("pair"),
        P(),
    )
    out_specs = P("pair", None, "virt")
    return jax.shard_map(local, mesh=mesh, in_specs=in_specs, out_specs=out_specs, check_vma=False)
```

```python
import functools

import jax
import jax.numpy as jnp
from jax import lax
from jax.experimental import pallas as pl
from jax.experimental.pallas import tpu as pltpu
from jax.sharding import PartitionSpec as P

VTILE = 32
MESH = pl.DeviceIdType.MESH
LANES = 128
LAG_RELAY, LAG_DOT, LAG_SEND = 3, 6, 7


def plan_kernel(local_rows, pair_map, amp_pairs, block_cols, tile_of_slot, meta):
    slots = tile_of_slot.shape[0]

    def clear(d, carry):
        tile_of_slot[d] = 0
        meta[0, 0, d] = -1
        return carry

    lax.fori_loop(0, slots, clear, 0)

    def place(j, carry):
        row = pair_map[amp_pairs[j]]

        @pl.when(row >= 0)
        def _():
            owner = lax.div(row, local_rows)
            tile_of_slot[owner] = j
            meta[0, 0, owner] = lax.rem(row, local_rows)

        return carry

    lax.fori_loop(0, amp_pairs.shape[0], place, 0)

    def copy(i, carry):
        meta[0, 0, slots + i] = block_cols[i]
        return carry

    lax.fori_loop(0, block_cols.shape[0], copy, 0)


def exchange_kernel(
    dims,
    tile_of_slot,
    meta_in,
    amplitudes,
    integrals,
    returned,
    meta_all,
    targets,
    slots,
    gathered,
    blocks,
    products,
    meta_table,
    amp_send,
    amp_recv,
    right_send,
    left_send,
    relay_right_send,
    relay_left_send,
    from_left,
    from_right,
    relay_from_left,
    relay_from_right,
    product_send,
    product_recv,
    meta_send,
    meta_recv,
    load_sem,
):
    ny, nz, nc = dims
    n = ny * nz * nc
    me = lax.axis_index("pair")
    col = lax.axis_index("virt")
    nv = gathered.shape[1]
    height = gathered.shape[2]
    half = height // 2
    right, left, across = lax.rem(col + 1, nv), lax.rem(col + nv - 1, nv), lax.rem(col + 2, nv)
    my_y, my_z, my_c = lax.div(me, nz * nc), lax.rem(lax.div(me, nc), nz), lax.rem(me, nc)

    def partner(k, sign):
        i = lax.rem(k, nz)
        t = lax.div(i + 1, 2)
        odd = lax.rem(i, 2)
        dz = odd * t + (1 - odd) * lax.rem(nz - t, nz)
        dy = lax.rem(lax.div(k, nz), ny)
        dc = lax.div(k, nz * ny)
        y = lax.rem(my_y + sign * dy + ny, ny)
        z = lax.rem(my_z + sign * dz + nz, nz)
        c = lax.rem(my_c + dc, nc)
        return (y * nz + z) * nc + c

    def wait(ref, sem):
        pltpu.make_async_copy(ref, ref, sem).wait()

    load = pltpu.make_async_copy(integrals, blocks, load_sem)
    load.start()

    barrier = pltpu.get_barrier_semaphore()

    def greet(k, carry):
        pl.semaphore_signal(barrier, inc=1, device_id=(partner(k, 1), col), device_id_type=MESH)
        return carry

    lax.fori_loop(1, n, greet, 0)
    pl.semaphore_signal(barrier, inc=1, device_id=(me, right), device_id_type=MESH)
    pl.semaphore_signal(barrier, inc=1, device_id=(me, left), device_id_type=MESH)

    def fill(d, carry):
        slots[d] = amplitudes[tile_of_slot[d]]
        return carry

    lax.fori_loop(0, n, fill, 0)

    pl.semaphore_wait(barrier, n + 1)

    def send_meta(k, carry):
        pltpu.make_async_remote_copy(
            src_ref=meta_in.at[0],
            dst_ref=meta_all.at[me],
            send_sem=meta_send,
            recv_sem=meta_recv,
            device_id=(partner(k, 1), col),
            device_id_type=MESH,
        ).start()
        return carry

    lax.fori_loop(1, n, send_meta, 0)
    pltpu.make_async_copy(meta_in.at[0], meta_all.at[me], meta_recv).start()
    pltpu.make_async_copy(slots.at[me], gathered.at[me, col], amp_recv.at[0]).start()

    def send_slot(k, carry):
        target = partner(k, 1)
        pltpu.make_async_remote_copy(
            src_ref=slots.at[target],
            dst_ref=gathered.at[me, col],
            send_sem=amp_send,
            recv_sem=amp_recv.at[k],
            device_id=(target, col),
            device_id_type=MESH,
        ).start()
        return carry

    lax.fori_loop(1, n, send_slot, 0)

    wait(meta_all, meta_recv)
    table = pltpu.make_async_copy(meta_all, meta_table, load_sem)
    load.wait()
    table.start()
    table.wait()

    def along(ref, send_sem, recv_sem, target):
        pltpu.make_async_remote_copy(
            src_ref=ref,
            dst_ref=ref,
            send_sem=send_sem,
            recv_sem=recv_sem,
            device_id=(me, target),
            device_id_type=MESH,
        ).start()

    def step(t, carry):
        @pl.when(t < n)
        def _():
            own = gathered.at[partner(t, -1), col]
            wait(own, amp_recv.at[t])
            along(own, right_send, from_left.at[t], right)
            along(own, left_send, from_right.at[t], left)

        @pl.when((t >= LAG_RELAY) & (t < n + LAG_RELAY))
        def _():
            u = t - LAG_RELAY
            source = partner(u, -1)
            wait(gathered.at[source, left], from_left.at[u])
            along(
                gathered.at[source, left, pl.ds(0, half)], relay_right_send, relay_from_left.at[u], right
            )
            wait(gathered.at[source, right], from_right.at[u])
            along(
                gathered.at[source, right, pl.ds(half, half)], relay_left_send, relay_from_right.at[u], left
            )

        @pl.when((t >= LAG_DOT) & (t < n + LAG_DOT))
        def _():
            u = t - LAG_DOT
            source = partner(u, -1)
            wait(gathered.at[source, across, pl.ds(0, half)], relay_from_left.at[u])
            wait(gathered.at[source, across, pl.ds(half, half)], relay_from_right.at[u])
            row = jnp.maximum(meta_table[source, 0, me], 0)
            tile = gathered[source].reshape(nv * height, gathered.shape[3])
            for m in range(blocks.shape[1]):
                products[u, m] = jnp.dot(
                    tile, blocks[row, m], preferred_element_type=jnp.float32
                ).astype(jnp.bfloat16)

        @pl.when(t == LAG_SEND)
        def _():
            pltpu.make_async_copy(products.at[0], returned.at[me], product_recv).start()

        @pl.when(t > LAG_SEND)
        def _():
            u = t - LAG_SEND
            pltpu.make_async_remote_copy(
                src_ref=products.at[u],
                dst_ref=returned.at[me],
                send_sem=product_send,
                recv_sem=product_recv,
                device_id=(partner(u, -1), col),
                device_id_type=MESH,
            ).start()

        return carry

    lax.fori_loop(0, n + LAG_SEND, step, 0)

    block_count = blocks.shape[1]

    def find_targets(d, carry):
        row = meta_table[me, 0, d]
        for m in range(block_count):
            pair = meta_table[d, 0, n + jnp.maximum(row, 0) * block_count + m]
            targets[d * block_count + m] = jnp.where(row >= 0, pair, -1)
        return carry

    lax.fori_loop(0, n, find_targets, 0)

    wait(meta_all.at[pl.ds(0, n - 1)], meta_send)
    wait(slots.at[pl.ds(0, n - 1)], amp_send)
    wait(slots, right_send)
    wait(slots, left_send)
    wait(slots.at[pl.ds(0, n // 2)], relay_right_send)
    wait(slots.at[pl.ds(0, n // 2)], relay_left_send)
    wait(products.at[pl.ds(0, n - 1)], product_send)
    wait(returned, product_recv)


def combine_kernel(
    virt_tiles, amp_pairs, targets, returned, first_table, second_table, occ, update, position, ladder
):
    step = pl.program_id(0)
    chunk = returned.shape[0]

    @pl.when(step == 0)
    def _():
        def mark(j, carry):
            position[amp_pairs[j]] = j
            return carry

        lax.fori_loop(0, amp_pairs.shape[0], mark, 0)
        ladder[...] = jnp.zeros_like(ladder)

    def add(i, carry):
        first = (step * chunk + i) * returned.shape[1]

        @pl.when(targets[first] >= 0)
        def _():
            for m in range(returned.shape[1]):
                ladder[position[targets[first + m]]] += returned[i, m].astype(jnp.float32)

        return carry

    lax.fori_loop(0, chunk, add, 0)

    @pl.when(step == pl.num_programs(0) - 1)
    def _():
        def divide(j, carry):
            pair = amp_pairs[j]
            energy = (
                first_table[pl.ds(lax.div(pair, virt_tiles), 1), :]
                + second_table[pl.ds(lax.rem(pair, virt_tiles), 1), :]
            )
            update[j] = (ladder[j] / (energy - occ[...])).astype(update.dtype)
            return carry

        lax.fori_loop(0, amp_pairs.shape[0], divide, 0)


def pair_dims(n):
    return {64: (4, 8, 2), 8: (2, 2, 2), 4: (1, 2, 2)}[n]


def local(amplitudes, amp_pairs, pair_map, integrals, block_cols, occ_energy, virt_energy):
    tile_count, height, full_width = amplitudes.shape
    n = lax.axis_size("pair")
    nv = lax.axis_size("virt")
    local_rows, block_count, _, part_width = integrals.shape
    occ_rows = occ_energy.shape[0]
    smem = pl.BlockSpec(memory_space=pltpu.SMEM)
    vmem = pl.BlockSpec(memory_space=pltpu.VMEM)
    hbm = pl.BlockSpec(memory_space=pl.ANY)

    tile_of_slot, my_meta = pl.pallas_call(
        functools.partial(plan_kernel, local_rows),
        out_shape=(
            jax.ShapeDtypeStruct((n,), jnp.int32),
            jax.ShapeDtypeStruct((1, 1, LANES), jnp.int32),
        ),
        in_specs=[smem] * 3,
        out_specs=(smem, smem),
        name="plan",
    )(pair_map, amp_pairs, block_cols.reshape(-1))

    dma = pltpu.SemaphoreType.DMA
    returned, _, targets = pl.pallas_call(
        functools.partial(exchange_kernel, pair_dims(n)),
        out_shape=(
            jax.ShapeDtypeStruct((n, block_count, occ_rows, part_width), jnp.bfloat16),
            jax.ShapeDtypeStruct((n, 1, LANES), jnp.int32),
            jax.ShapeDtypeStruct((n * block_count,), jnp.int32),
        ),
        in_specs=[smem, vmem, vmem, hbm],
        out_specs=(hbm, hbm, smem),
        scratch_shapes=[
            pltpu.VMEM((n, height, full_width), jnp.bfloat16),
            pltpu.VMEM((n, nv, height, full_width), jnp.bfloat16),
            pltpu.VMEM(integrals.shape, jnp.bfloat16),
            pltpu.VMEM((n, block_count, occ_rows, part_width), jnp.bfloat16),
            pltpu.SMEM((n, 1, LANES), jnp.int32),
            dma,
            dma((n,)),
            dma,
            dma,
            dma,
            dma,
            dma((n,)),
            dma((n,)),
            dma((n,)),
            dma((n,)),
            dma,
            dma,
            dma,
            dma,
            dma,
        ],
        compiler_params=pltpu.CompilerParams(
            collective_id=0, has_side_effects=True, vmem_limit_bytes=60 * 2**20
        ),
        name="exchange",
    )(tile_of_slot, my_meta, amplitudes, integrals)

    virt_tiles = virt_energy.shape[0] // VTILE
    energy_table = virt_energy.reshape(virt_tiles, VTILE)
    per_device = VTILE // nv
    first = lax.dynamic_slice_in_dim(
        energy_table, lax.axis_index("virt") * per_device, per_device, 1
    )
    first_table = jnp.repeat(first, VTILE, axis=1)
    second_table = jnp.tile(energy_table, (1, per_device))
    chunk = min(8, n)
    whole = lambda *shape: pl.BlockSpec(shape, lambda i: (0,) * len(shape))
    return pl.pallas_call(
        functools.partial(combine_kernel, virt_tiles),
        out_shape=jax.ShapeDtypeStruct((tile_count, occ_rows, part_width), jnp.bfloat16),
        grid=(n // chunk,),
        in_specs=[
            smem,
            smem,
            pl.BlockSpec((chunk, block_count, occ_rows, part_width), lambda i: (i, 0, 0, 0)),
            whole(virt_tiles, part_width),
            whole(virt_tiles, part_width),
            whole(occ_rows, 1),
        ],
        out_specs=whole(tile_count, occ_rows, part_width),
        scratch_shapes=[
            pltpu.SMEM((pair_map.shape[0],), jnp.int32),
            pltpu.VMEM((tile_count, occ_rows, part_width), jnp.float32),
        ],
        compiler_params=pltpu.CompilerParams(vmem_limit_bytes=32 * 2**20),
        name="combine",
    )(amp_pairs, targets, returned, first_table, second_table, occ_energy[:, None])


def solution(mesh):
    in_specs = (
        P("pair", "virt", None),
        P("pair"),
        P(),
        P("pair", None, None, "virt"),
        P("pair", None),
        P("pair"),
        P(),
    )
    out_specs = P("pair", None, "virt")
    return jax.shard_map(local, mesh=mesh, in_specs=in_specs, out_specs=out_specs, check_vma=False)
```

```python
import functools

import jax
import jax.numpy as jnp
from jax import lax
from jax.experimental import pallas as pl
from jax.experimental.pallas import tpu as pltpu
from jax.sharding import PartitionSpec as P

VTILE = 32
MESH = pl.DeviceIdType.MESH
LANES = 128
LAG_RELAY, LAG_DOT, LAG_SEND = 3, 6, 7


def plan_kernel(local_rows, pair_map, amp_pairs, block_cols, tile_of_slot, meta):
    slots = tile_of_slot.shape[0]

    def clear(d, carry):
        tile_of_slot[d] = 0
        meta[0, 0, d] = -1
        return carry

    lax.fori_loop(0, slots, clear, 0, unroll=8)

    def place(j, carry):
        row = pair_map[amp_pairs[j]]

        @pl.when(row >= 0)
        def _():
            owner = lax.div(row, local_rows)
            tile_of_slot[owner] = j
            meta[0, 0, owner] = lax.rem(row, local_rows)

        return carry

    lax.fori_loop(0, amp_pairs.shape[0], place, 0, unroll=8)

    def copy(i, carry):
        meta[0, 0, slots + i] = block_cols[i]
        return carry

    lax.fori_loop(0, block_cols.shape[0], copy, 0, unroll=8)


def exchange_kernel(
    dims,
    tile_of_slot,
    meta_in,
    amplitudes,
    integrals,
    returned,
    meta_all,
    targets,
    slots,
    gathered,
    blocks,
    products,
    meta_table,
    amp_send,
    amp_recv,
    right_send,
    left_send,
    relay_right_send,
    relay_left_send,
    from_left,
    from_right,
    relay_from_left,
    relay_from_right,
    product_send,
    product_recv,
    meta_send,
    meta_recv,
    load_sem,
):
    ny, nz, nc = dims
    n = ny * nz * nc
    me = lax.axis_index("pair")
    col = lax.axis_index("virt")
    nv = gathered.shape[1]
    height = gathered.shape[2]
    half = height // 2
    right, left, across = lax.rem(col + 1, nv), lax.rem(col + nv - 1, nv), lax.rem(col + 2, nv)
    my_y, my_z, my_c = lax.div(me, nz * nc), lax.rem(lax.div(me, nc), nz), lax.rem(me, nc)

    def partner(k, sign):
        i = lax.rem(k, nz)
        t = lax.div(i + 1, 2)
        odd = lax.rem(i, 2)
        dz = odd * t + (1 - odd) * lax.rem(nz - t, nz)
        dy = lax.rem(lax.div(k, nz), ny)
        dc = lax.div(k, nz * ny)
        y = lax.rem(my_y + sign * dy + ny, ny)
        z = lax.rem(my_z + sign * dz + nz, nz)
        c = lax.rem(my_c + dc, nc)
        return (y * nz + z) * nc + c

    def wait(ref, sem):
        pltpu.make_async_copy(ref, ref, sem).wait()

    load = pltpu.make_async_copy(integrals, blocks, load_sem)
    load.start()

    barrier = pltpu.get_barrier_semaphore()

    def greet(k, carry):
        pl.semaphore_signal(barrier, inc=1, device_id=(partner(k, 1), col), device_id_type=MESH)
        return carry

    lax.fori_loop(1, n, greet, 0)
    pl.semaphore_signal(barrier, inc=1, device_id=(me, right), device_id_type=MESH)
    pl.semaphore_signal(barrier, inc=1, device_id=(me, left), device_id_type=MESH)

    def fill(d, carry):
        slots[d] = amplitudes[tile_of_slot[d]]
        return carry

    lax.fori_loop(0, n, fill, 0)

    pl.semaphore_wait(barrier, n + 1)

    def send_meta(k, carry):
        pltpu.make_async_remote_copy(
            src_ref=meta_in.at[0],
            dst_ref=meta_all.at[me],
            send_sem=meta_send,
            recv_sem=meta_recv,
            device_id=(partner(k, 1), col),
            device_id_type=MESH,
        ).start()
        return carry

    lax.fori_loop(1, n, send_meta, 0)
    pltpu.make_async_copy(meta_in.at[0], meta_all.at[me], meta_recv).start()
    pltpu.make_async_copy(slots.at[me], gathered.at[me, col], amp_recv.at[0]).start()

    def send_slot(k, carry):
        target = partner(k, 1)
        pltpu.make_async_remote_copy(
            src_ref=slots.at[target],
            dst_ref=gathered.at[me, col],
            send_sem=amp_send,
            recv_sem=amp_recv.at[k],
            device_id=(target, col),
            device_id_type=MESH,
        ).start()
        return carry

    lax.fori_loop(1, n, send_slot, 0)

    wait(meta_all, meta_recv)
    table = pltpu.make_async_copy(meta_all, meta_table, load_sem)
    load.wait()
    table.start()
    table.wait()

    def along(ref, send_sem, recv_sem, target):
        pltpu.make_async_remote_copy(
            src_ref=ref,
            dst_ref=ref,
            send_sem=send_sem,
            recv_sem=recv_sem,
            device_id=(me, target),
            device_id_type=MESH,
        ).start()

    def step(t, carry):
        @pl.when(t < n)
        def _():
            own = gathered.at[partner(t, -1), col]
            wait(own, amp_recv.at[t])
            along(own, right_send, from_left.at[t], right)
            along(own, left_send, from_right.at[t], left)

        @pl.when((t >= LAG_RELAY) & (t < n + LAG_RELAY))
        def _():
            u = t - LAG_RELAY
            source = partner(u, -1)
            wait(gathered.at[source, left], from_left.at[u])
            along(
                gathered.at[source, left, pl.ds(0, half)], relay_right_send, relay_from_left.at[u], right
            )
            wait(gathered.at[source, right], from_right.at[u])
            along(
                gathered.at[source, right, pl.ds(half, half)], relay_left_send, relay_from_right.at[u], left
            )

        @pl.when((t >= LAG_DOT) & (t < n + LAG_DOT))
        def _():
            u = t - LAG_DOT
            source = partner(u, -1)
            wait(gathered.at[source, across, pl.ds(0, half)], relay_from_left.at[u])
            wait(gathered.at[source, across, pl.ds(half, half)], relay_from_right.at[u])
            row = jnp.maximum(meta_table[source, 0, me], 0)
            tile = gathered[source].reshape(nv * height, gathered.shape[3])
            for m in range(blocks.shape[1]):
                products[u, m] = jnp.dot(
                    tile, blocks[row, m], preferred_element_type=jnp.float32
                ).astype(jnp.bfloat16)

        @pl.when(t == LAG_SEND)
        def _():
            pltpu.make_async_copy(products.at[0], returned.at[me], product_recv).start()

        @pl.when(t > LAG_SEND)
        def _():
            u = t - LAG_SEND
            pltpu.make_async_remote_copy(
                src_ref=products.at[u],
                dst_ref=returned.at[me],
                send_sem=product_send,
                recv_sem=product_recv,
                device_id=(partner(u, -1), col),
                device_id_type=MESH,
            ).start()

        return carry

    lax.fori_loop(0, n + LAG_SEND, step, 0)

    block_count = blocks.shape[1]

    def find_targets(d, carry):
        row = meta_table[me, 0, d]
        for m in range(block_count):
            pair = meta_table[d, 0, n + jnp.maximum(row, 0) * block_count + m]
            targets[d * block_count + m] = jnp.where(row >= 0, pair, -1)
        return carry

    lax.fori_loop(0, n, find_targets, 0)

    wait(meta_all.at[pl.ds(0, n - 1)], meta_send)
    wait(slots.at[pl.ds(0, n - 1)], amp_send)
    wait(slots, right_send)
    wait(slots, left_send)
    wait(slots.at[pl.ds(0, n // 2)], relay_right_send)
    wait(slots.at[pl.ds(0, n // 2)], relay_left_send)
    wait(products.at[pl.ds(0, n - 1)], product_send)
    wait(returned, product_recv)


def combine_kernel(
    virt_tiles, amp_pairs, targets, returned, first_table, second_table, occ, update, position, ladder
):
    step = pl.program_id(0)
    chunk = returned.shape[0]

    @pl.when(step == 0)
    def _():
        def mark(j, carry):
            position[amp_pairs[j]] = j
            return carry

        lax.fori_loop(0, amp_pairs.shape[0], mark, 0, unroll=8)
        ladder[...] = jnp.zeros_like(ladder)

    def add(i, carry):
        first = (step * chunk + i) * returned.shape[1]

        @pl.when(targets[first] >= 0)
        def _():
            for m in range(returned.shape[1]):
                ladder[position[targets[first + m]]] += returned[i, m].astype(jnp.float32)

        return carry

    lax.fori_loop(0, chunk, add, 0)

    @pl.when(step == pl.num_programs(0) - 1)
    def _():
        rows = occ.shape[1]
        occ_column = jnp.transpose(jnp.broadcast_to(occ[...], (rows, rows)))[:, :1]

        def divide(j, carry):
            pair = amp_pairs[j]
            energy = (
                first_table[pl.ds(lax.div(pair, virt_tiles), 1), :]
                + second_table[pl.ds(lax.rem(pair, virt_tiles), 1), :]
            )
            update[j] = (ladder[j] / (energy - occ_column)).astype(update.dtype)
            return carry

        lax.fori_loop(0, amp_pairs.shape[0], divide, 0)


def pair_dims(n):
    return {64: (4, 8, 2), 8: (2, 2, 2), 4: (1, 2, 2)}[n]


def local(amplitudes, amp_pairs, pair_map, integrals, block_cols, occ_energy, virt_energy):
    tile_count, height, full_width = amplitudes.shape
    n = lax.axis_size("pair")
    nv = lax.axis_size("virt")
    local_rows, block_count, _, part_width = integrals.shape
    occ_rows = occ_energy.shape[0]
    smem = pl.BlockSpec(memory_space=pltpu.SMEM)
    vmem = pl.BlockSpec(memory_space=pltpu.VMEM)
    hbm = pl.BlockSpec(memory_space=pl.ANY)

    tile_of_slot, my_meta = pl.pallas_call(
        functools.partial(plan_kernel, local_rows),
        out_shape=(
            jax.ShapeDtypeStruct((n,), jnp.int32),
            jax.ShapeDtypeStruct((1, 1, LANES), jnp.int32),
        ),
        in_specs=[smem] * 3,
        out_specs=(smem, smem),
        name="plan",
    )(pair_map, amp_pairs, block_cols.reshape(-1))

    dma = pltpu.SemaphoreType.DMA
    returned, _, targets = pl.pallas_call(
        functools.partial(exchange_kernel, pair_dims(n)),
        out_shape=(
            jax.ShapeDtypeStruct((n, block_count, occ_rows, part_width), jnp.bfloat16),
            jax.ShapeDtypeStruct((n, 1, LANES), jnp.int32),
            jax.ShapeDtypeStruct((n * block_count,), jnp.int32),
        ),
        in_specs=[smem, vmem, vmem, hbm],
        out_specs=(hbm, hbm, smem),
        scratch_shapes=[
            pltpu.VMEM((n, height, full_width), jnp.bfloat16),
            pltpu.VMEM((n, nv, height, full_width), jnp.bfloat16),
            pltpu.VMEM(integrals.shape, jnp.bfloat16),
            pltpu.VMEM((n, block_count, occ_rows, part_width), jnp.bfloat16),
            pltpu.SMEM((n, 1, LANES), jnp.int32),
            dma,
            dma((n,)),
            dma,
            dma,
            dma,
            dma,
            dma((n,)),
            dma((n,)),
            dma((n,)),
            dma((n,)),
            dma,
            dma,
            dma,
            dma,
            dma,
        ],
        compiler_params=pltpu.CompilerParams(
            collective_id=0, has_side_effects=True, vmem_limit_bytes=60 * 2**20
        ),
        name="exchange",
    )(tile_of_slot, my_meta, amplitudes, integrals)

    virt_tiles = virt_energy.shape[0] // VTILE
    energy_table = virt_energy.reshape(virt_tiles, VTILE)
    per_device = VTILE // nv
    first = lax.dynamic_slice_in_dim(
        energy_table, lax.axis_index("virt") * per_device, per_device, 1
    )
    first_table = jnp.repeat(first, VTILE, axis=1)
    second_table = jnp.tile(energy_table, (1, per_device))
    chunk = min(8, n)
    whole = lambda *shape: pl.BlockSpec(shape, lambda i: (0,) * len(shape))
    return pl.pallas_call(
        functools.partial(combine_kernel, virt_tiles),
        out_shape=jax.ShapeDtypeStruct((tile_count, occ_rows, part_width), jnp.bfloat16),
        grid=(n // chunk,),
        in_specs=[
            smem,
            smem,
            pl.BlockSpec((chunk, block_count, occ_rows, part_width), lambda i: (i, 0, 0, 0)),
            whole(virt_tiles, part_width),
            whole(virt_tiles, part_width),
            whole(1, occ_rows),
        ],
        out_specs=whole(tile_count, occ_rows, part_width),
        scratch_shapes=[
            pltpu.SMEM((pair_map.shape[0],), jnp.int32),
            pltpu.VMEM((tile_count, occ_rows, part_width), jnp.float32),
        ],
        compiler_params=pltpu.CompilerParams(vmem_limit_bytes=60 * 2**20),
        name="combine",
    )(amp_pairs, targets, returned, first_table, second_table, occ_energy[None, :])


def solution(mesh):
    in_specs = (
        P("pair", "virt", None),
        P("pair"),
        P(),
        P("pair", None, None, "virt"),
        P("pair", None),
        P("pair"),
        P(),
    )
    out_specs = P("pair", None, "virt")
    return jax.shard_map(local, mesh=mesh, in_specs=in_specs, out_specs=out_specs, check_vma=False)
```
